32 devices in a mesh: rec: 4 (over y, core), tm: 8 (over z, x).
Axes of the slice: x: 2, y: 2, z: 4, core: 2. Of those that a mesh axis runs over, the one named last changes fastest.
Arguments:
- loader_rows: bfloat16 [4, 16384, 1024], P('rec', 'tm'), may hold values from -6 to 6
- frame_counts: int32 [4, 8, 8], P('rec'), may hold values from 0 to 256, as said below
- lengths: int32 [4], P('rec'), may hold values from 4097 to 8192, as said below
- cotangent: bfloat16 [4, 8192, 1024], P('rec', 'tm'), may hold values from -6 to 6
- norm_gain: float32 [1024], replicated, may hold values from 0.5 to 1.5
- w_expand: bfloat16 [1024, 2048], replicated, may hold values from -0.1875 to 0.1875
- conv_taps: float32 [9, 1024], replicated, may hold values from -2 to 2
- conv_gain: float32 [1024], replicated, may hold values from 0.5 to 1.5
- w_project: bfloat16 [1024, 1024], replicated, may hold values from -0.1875 to 0.1875
Outputs:
- layer_out: bfloat16 [4, 8192, 1024], P('rec', 'tm')
- grad_in: bfloat16 [4, 8192, 1024], P('rec', 'tm')
- grad_expand: float32 [1024, 2048], P('tm')
- grad_project: float32 [1024, 1024], P('tm')
- grad_taps: float32 [9, 1024], replicated
- grad_norm_gain: float32 [1024], replicated
- grad_conv_gain: float32 [1024], replicated
The draws below stay inside these ranges and needn't reach their ends.
Inputs may be any that keep to these rules, and one draw needn't show every extreme that they name: frame_counts[r, j, k] rows of bucket (j, k) are live, in its first slots; the other slots hold values that are not part of the recording. For every r and k the counts sum over j to exactly 1024, and in every such column some source fills its bucket with 256 rows. `lengths`: in every draw some recording has all 8192 frames.
All inputs are finite; a program needn't handle non-finite values.
Results may differ from the reference program's by a relative error of at most 0.0062.
Values may be sent and summed in bfloat16 or wider, within the bound.
No kernel may reach another device: no remote copies, remote signals or barrier semaphores. Data moves between devices by JAX's collectives and lax.ppermute only.
A program may use at most 128 MiB of HBM per device.

```python
import jax
import jax.numpy as jnp
from jax import lax

D = 1024
KER = 9
FR_DEV = 1024
SHARDS = 8
RECS = 4
CAP = 256
NT = 8192


def draw_frame_counts(key, part):
    middle = FR_DEV // SHARDS
    spread = jax.random.randint(jax.random.fold_in(key, 11), (RECS, SHARDS, SHARDS // 2), 0, middle + 1)
    spread = spread.at[:, :, 0].set(middle)
    paired = jnp.stack([middle + spread, middle - spread], axis=-1).reshape(RECS, SHARDS, SHARDS)
    scores = jax.random.randint(jax.random.fold_in(key, 12), (RECS, SHARDS, SHARDS), 0, 1 << 20) * SHARDS
    scores = scores + jnp.arange(SHARDS, dtype=jnp.int32)
    ranking = jnp.argsort(scores, axis=-1, stable=True)
    shuffled = jnp.take_along_axis(paired, ranking, axis=-1)
    return jnp.transpose(shuffled, (0, 2, 1)).astype(jnp.int32)


def draw_lengths(key, part):
    frames_all = FR_DEV * SHARDS
    shortfall = jax.random.randint(jax.random.fold_in(key, 21), (RECS,), 0, frames_all // 2)
    longest = jax.random.randint(jax.random.fold_in(key, 22), (), 0, RECS)
    return jnp.where(jnp.arange(RECS) == longest, frames_all, frames_all - shortfall).astype(jnp.int32)


def strengthened(entries, own_key, source, target, blocks, factor):
    owner, partner = [(jnp.arange(entries.shape[axis_at]) // (entries.shape[axis_at] // blocks)).reshape([-1 if axis == axis_at else 1 for axis in range(entries.ndim)]) for axis_at in (source, target)]
    chosen = jax.random.permutation(own_key, blocks)[partner]
    strong = (owner == chosen) | (owner == (partner + blocks // 2) % blocks)
    return jnp.where(strong, factor * entries, entries)


def block_scale(stream_key, extent, split, least, largest):
    loudness = 1.0
    for dim, shards_of in split:
        heights = jax.random.uniform(jax.random.fold_in(jax.random.fold_in(stream_key, 6), dim), (shards_of,), jnp.float32, least / len(split), largest / len(split))
        loudness = loudness * jnp.repeat(jnp.exp(heights), extent[dim] // shards_of).reshape((-1,) + (1,) * (len(extent) - 1 - dim))
    return loudness


def normal_values(rng, shape, scale, reach, split=(), kind=jnp.bfloat16):
    values = scale * jax.random.normal(rng, shape, jnp.float32)
    if split:
        values = values * block_scale(rng, shape, split, -0.22, 0.18)
    return jnp.clip(values, -reach, reach).astype(kind)


def bell_draw_with(key, extent, scale, most, split, heavy, kind=jnp.bfloat16):
    drawn = scale * jax.random.normal(key, extent, jnp.float32)
    if split:
        drawn = drawn * block_scale(key, extent, split, -0.22, 0.18)
    return jnp.clip(strengthened(drawn, jax.random.fold_in(key, 3), *heavy), -most, most).astype(kind)


def setup_inputs(seed: int = 0) -> dict:
    splits = jax.random.split(jax.random.key(seed), 10)
    loader_rows = bell_draw_with(splits[0], (RECS, SHARDS * SHARDS * CAP, D), 1.0, 6.0, ((0, 4), (1, 8)), (1, 2, 8, 2.0))
    frame_counts = draw_frame_counts(jax.random.fold_in(splits[9], 71), 0)
    lengths = draw_lengths(jax.random.fold_in(splits[9], 71), 0)
    cotangent = normal_values(splits[3], (RECS, NT, D), 1.0, 6.0, ((0, 4), (1, 8)))
    norm_gain = jnp.clip(1.0 + 0.1 * jax.random.normal(splits[4], (D,), jnp.float32), 0.5, 1.5)
    w_expand = normal_values(splits[5], (D, 2 * D), D ** -0.5, 0.1875)
    conv_taps = normal_values(splits[6], (KER, D), KER ** -0.5, 2.0, (), jnp.float32)
    conv_gain = jnp.clip(1.0 + 0.1 * jax.random.normal(splits[7], (D,), jnp.float32), 0.5, 1.5)
    w_project = normal_values(splits[8], (D, D), D ** -0.5, 0.1875)
    return dict(loader_rows=loader_rows, frame_counts=frame_counts, lengths=lengths, cotangent=cotangent, norm_gain=norm_gain, w_expand=w_expand, conv_taps=conv_taps, conv_gain=conv_gain, w_project=w_project)


EPS = 1e-05

def normalize(values):
    center = values - lax.optimization_barrier(jnp.mean(values, axis=-1, keepdims=True))
    inverse = lax.rsqrt(lax.optimization_barrier(jnp.mean(center * center, axis=-1, keepdims=True)) + EPS)
    return (center * inverse, inverse)

def norm_back(grad_norm, normed, inverse):
    return inverse * (grad_norm - lax.optimization_barrier(jnp.mean(grad_norm, axis=-1, keepdims=True)) - normed * lax.optimization_barrier(jnp.mean(grad_norm * normed, axis=-1, keepdims=True)))

def contract_rows(left, right):
    return lax.dot_general(left, right, (((0,), (0,)), ((), ())), preferred_element_type=jnp.float32)

def contract_cols(left, right):
    return lax.dot_general(left, right, (((1,), (1,)), ((), ())), preferred_element_type=jnp.float32)

def regroup_record(loader_rec, counts_rec):
    run_ends = jnp.cumsum(counts_rec, axis=0).astype(jnp.int32)
    starts = (run_ends - counts_rec).astype(jnp.int32)
    position = jnp.arange(FR_DEV, dtype=jnp.int32)
    source = lax.optimization_barrier(jnp.sum((run_ends[:, :, None] <= position[None, None, :]).astype(jnp.int32), axis=0))
    first_slot = jnp.take_along_axis(starts, source.T, axis=0).T
    shard_ids = jnp.arange(SHARDS, dtype=jnp.int32)[:, None]
    row_index = source * (SHARDS * CAP) + shard_ids * CAP + position[None, :] - first_slot
    return loader_rec[row_index.reshape(-1).astype(jnp.int32)]

def layer(sequence, valid_mask, cotangent, norm_gain, w_expand, conv_taps, conv_gain, w_project):
    frames = sequence.shape[0]
    channels = sequence.shape[1]
    taps_count = conv_taps.shape[0]
    margin = taps_count // 2
    inputs = sequence.astype(jnp.float32)
    normed_in, inverse_in = normalize(inputs)
    scaled_in = (normed_in * norm_gain).astype(jnp.bfloat16)
    expanded = jnp.dot(scaled_in, w_expand, preferred_element_type=jnp.float32)
    linear = expanded[:, :channels]
    gate_sig = jax.nn.sigmoid(expanded[:, channels:])
    glu_out = (linear * gate_sig * valid_mask).astype(jnp.bfloat16)
    glu_rim = jnp.pad(glu_out, ((margin, margin), (0, 0)))
    depthwise = jnp.zeros((frames, channels), jnp.float32)
    for kernel_tap in range(taps_count):
        depthwise = depthwise + conv_taps[kernel_tap] * glu_rim[kernel_tap:kernel_tap + frames].astype(jnp.float32)
    normed_conv, inverse_conv = normalize(depthwise)
    scaled_conv = normed_conv * conv_gain
    swish_sig = jax.nn.sigmoid(scaled_conv)
    swished = (scaled_conv * swish_sig).astype(jnp.bfloat16)
    projected = jnp.dot(swished, w_project, preferred_element_type=jnp.float32)
    layer_out = ((inputs + projected) * valid_mask).astype(jnp.bfloat16)
    grad_out = jnp.where(valid_mask > 0.5, cotangent, jnp.zeros_like(cotangent))
    grad_project = contract_rows(swished, grad_out)
    grad_swished = contract_cols(grad_out, w_project)
    grad_scaled_conv = grad_swished * swish_sig * (1.0 + scaled_conv * (1.0 - swish_sig))
    grad_conv_gain = lax.optimization_barrier(jnp.sum(grad_scaled_conv * normed_conv, axis=0))
    grad_depth = norm_back(grad_scaled_conv * conv_gain, normed_conv, inverse_conv)
    depth_rim = jnp.pad(grad_depth, ((margin, margin), (0, 0)))
    grad_taps = jnp.stack([lax.optimization_barrier(jnp.sum(grad_depth * glu_rim[kernel_tap:kernel_tap + frames].astype(jnp.float32), axis=0)) for kernel_tap in range(taps_count)])
    grad_glu = jnp.zeros((frames, channels), jnp.float32)
    for kernel_tap in range(taps_count):
        offset = 2 * margin - kernel_tap
        grad_glu = grad_glu + conv_taps[kernel_tap] * depth_rim[offset:offset + frames]
    grad_glu = grad_glu * valid_mask
    grad_expanded = jnp.concatenate([grad_glu * gate_sig, grad_glu * linear * gate_sig * (1.0 - gate_sig)], axis=1).astype(jnp.bfloat16)
    grad_expand = contract_rows(scaled_in, grad_expanded)
    grad_scaled_in = contract_cols(grad_expanded, w_expand)
    grad_norm_gain = lax.optimization_barrier(jnp.sum(grad_scaled_in * normed_in, axis=0))
    grad_in = (grad_out.astype(jnp.float32) + norm_back(grad_scaled_in * norm_gain, normed_in, inverse_in)).astype(jnp.bfloat16)
    return (layer_out, grad_in, grad_expand, grad_project, grad_taps, grad_norm_gain, grad_conv_gain)

def reference(loader_rows, frame_counts, lengths, cotangent, norm_gain, w_expand, conv_taps, conv_gain, w_project):
    frames_all = FR_DEV * SHARDS

    def one_record(carry, inputs):
        loader_rec, counts_rec, length, cot_rec = inputs
        sequence = regroup_record(loader_rec, counts_rec)
        valid_mask = (jnp.arange(frames_all, dtype=jnp.int32) < length).astype(jnp.float32)[:, None]
        result = layer(sequence, valid_mask, cot_rec, norm_gain, w_expand, conv_taps, conv_gain, w_project)
        carry = jax.tree.map(jnp.add, carry, tuple(result[2:]))
        return (carry, (result[0], result[1]))
    start = (jnp.zeros((D, 2 * D), jnp.float32), jnp.zeros((D, D), jnp.float32), jnp.zeros((KER, D), jnp.float32), jnp.zeros((D,), jnp.float32), jnp.zeros((D,), jnp.float32))
    sums, stacked = lax.scan(one_record, start, (loader_rows, frame_counts, lengths, cotangent))
    return (stacked[0], stacked[1], sums[0], sums[1], sums[2], sums[3], sums[4])
```

```python
import jax
import jax.numpy as jnp
from jax import lax
from jax.sharding import PartitionSpec as P

EPS = 1e-05


def with_halo(value, sides, width):
    for axis, dim in sides:
        size, length = (lax.axis_size(axis), value.shape[dim])
        up = [(i, (i + 1) % size) for i in range(size - 1)]
        down = [(j, i) for i, j in up]
        last = lax.slice_in_dim(value, length - width, length, axis=dim)
        first = lax.slice_in_dim(value, 0, width, axis=dim)
        before = lax.ppermute(last, axis, up)
        after = lax.ppermute(first, axis, down)
        value = jnp.concatenate([before, value, after], axis=dim)
    return value


def normalize(values):
    center = values - jnp.mean(values, axis=-1, keepdims=True)
    inverse = lax.rsqrt(jnp.mean(center * center, axis=-1, keepdims=True) + EPS)
    return (center * inverse, inverse)


def norm_back(grad_norm, normed, inverse):
    return inverse * (
        grad_norm
        - jnp.mean(grad_norm, axis=-1, keepdims=True)
        - normed * jnp.mean(grad_norm * normed, axis=-1, keepdims=True)
    )


def contract_rows(left, right):
    return lax.dot_general(
        left, right, (((0,), (0,)), ((), ())), preferred_element_type=jnp.float32
    )


def contract_cols(left, right):
    return lax.dot_general(
        left, right, (((1,), (1,)), ((), ())), preferred_element_type=jnp.float32
    )


def swap(value, axis, bit):
    size = lax.axis_size(axis)
    return lax.ppermute(value, axis, [(i, i ^ bit) for i in range(size)])


def bits_of(size):
    return [1 << b for b in range(size.bit_length() - 1)]


def fold_plans(recs, shards):
    rec_bits = [("rec", b) for b in bits_of(recs)]
    tm_bits = [("tm", b) for b in bits_of(shards)]
    first = rec_bits + tm_bits
    second = rec_bits[:1] + tm_bits[:1] + rec_bits[1:] + tm_bits[1:]
    return (first, second)


def fold(value, dim, axis, bit):
    mine = (lax.axis_index(axis) // bit) % 2
    other = lax.dynamic_index_in_dim(value, 1 - mine, dim, keepdims=False)
    arrived = swap(other.astype(jnp.bfloat16), axis, bit)
    return lax.dynamic_index_in_dim(value, mine, dim, keepdims=False) + arrived.astype(jnp.float32)


def sum_shares(partial, plan):
    recs, shards = lax.axis_size("rec"), lax.axis_size("tm")
    rows, columns = partial.shape
    block = rows // (recs * shards)
    left = [("tm", b) for b in reversed(bits_of(shards))]
    left += [("rec", b) for b in reversed(bits_of(recs))]
    value = partial.reshape((2,) * len(left) + (block, columns))
    for key in plan:
        value = fold(value, left.index(key), *key)
        left.remove(key)
    share = value.astype(jnp.bfloat16)[None]
    for bit in bits_of(recs):
        mine = (lax.axis_index("rec") // bit) % 2
        other = swap(share, "rec", bit)
        share = jnp.where(
            mine == 0,
            jnp.concatenate([share, other], axis=0),
            jnp.concatenate([other, share], axis=0),
        )
    return share.reshape(recs * block, columns).astype(jnp.float32)


def sum_everywhere(value):
    for axis in ("rec", "tm"):
        for bit in bits_of(lax.axis_size(axis)):
            value = value + swap(value, axis, bit)
    return value


def per_device(
    loader_rows,
    frame_counts,
    lengths,
    cotangent,
    norm_gain,
    w_expand,
    conv_taps,
    conv_gain,
    w_project,
):
    shards = lax.axis_size("tm")
    shard_index = lax.axis_index("tm")
    channels = norm_gain.shape[0]
    frames = cotangent.shape[1]
    capacity = loader_rows.shape[1] // shards
    taps_count = conv_taps.shape[0]
    margin = taps_count // 2
    buckets = loader_rows[0].reshape(shards, capacity, channels)
    arrived = lax.all_to_all(buckets, "tm", split_axis=0, concat_axis=0, tiled=True).reshape(
        shards * capacity, channels
    )
    shard_ids = jnp.arange(shards, dtype=jnp.int32)
    column = jnp.sum(jnp.where(shard_ids[None, :] == shard_index, frame_counts[0], 0), axis=1)
    run_ends = jnp.cumsum(column)
    starts = run_ends - column
    position = jnp.arange(frames, dtype=jnp.int32)
    source = jnp.sum((run_ends[:, None] <= position[None, :]).astype(jnp.int32), axis=0)
    picked = source[:, None] == shard_ids[None, :]
    first_slot = jnp.sum(jnp.where(picked, starts[None, :], 0), axis=1)
    row_index = source * capacity + position - first_slot
    sequence = jnp.take(arrived, row_index, axis=0)
    valid_mask = (shard_index * frames + position < lengths[0]).astype(jnp.float32)[:, None]
    inputs = sequence.astype(jnp.float32)
    normed_in, inverse_in = normalize(inputs)
    scaled_in = (normed_in * norm_gain).astype(jnp.bfloat16)
    expanded = jnp.dot(scaled_in, w_expand, preferred_element_type=jnp.float32)
    linear = expanded[:, :channels]
    gate_sig = jax.nn.sigmoid(expanded[:, channels:])
    glu_out = (linear * gate_sig * valid_mask).astype(jnp.bfloat16)
    glu_rim = with_halo(glu_out, (("tm", 0),), margin)
    depthwise = jnp.zeros((frames, channels), jnp.float32)
    for kernel_tap in range(taps_count):
        depthwise = depthwise + conv_taps[kernel_tap] * glu_rim[
            kernel_tap : kernel_tap + frames
        ].astype(jnp.float32)
    normed_conv, inverse_conv = normalize(depthwise)
    scaled_conv = normed_conv * conv_gain
    swish_sig = jax.nn.sigmoid(scaled_conv)
    swished = (scaled_conv * swish_sig).astype(jnp.bfloat16)
    projected = jnp.dot(swished, w_project, preferred_element_type=jnp.float32)
    layer_out = ((inputs + projected) * valid_mask).astype(jnp.bfloat16)
    cot_rec = cotangent[0]
    grad_out = jnp.where(valid_mask > 0.5, cot_rec, jnp.zeros_like(cot_rec))
    grad_project = contract_rows(swished, grad_out)
    grad_swished = contract_cols(grad_out, w_project)
    grad_scaled_conv = grad_swished * swish_sig * (1.0 + scaled_conv * (1.0 - swish_sig))
    grad_conv_gain = jnp.sum(grad_scaled_conv * normed_conv, axis=0)
    grad_depth = norm_back(grad_scaled_conv * conv_gain, normed_conv, inverse_conv)
    depth_rim = with_halo(grad_depth, (("tm", 0),), margin)
    grad_taps = jnp.stack(
        [
            jnp.sum(
                grad_depth * glu_rim[kernel_tap : kernel_tap + frames].astype(jnp.float32), axis=0
            )
            for kernel_tap in range(taps_count)
        ]
    )
    grad_glu = jnp.zeros((frames, channels), jnp.float32)
    for kernel_tap in range(taps_count):
        offset = 2 * margin - kernel_tap
        grad_glu = grad_glu + conv_taps[kernel_tap] * depth_rim[offset : offset + frames]
    grad_glu = grad_glu * valid_mask
    grad_expanded = jnp.concatenate(
        [grad_glu * gate_sig, grad_glu * linear * gate_sig * (1.0 - gate_sig)], axis=1
    ).astype(jnp.bfloat16)
    grad_expand = contract_rows(scaled_in, grad_expanded)
    grad_scaled_in = contract_cols(grad_expanded, w_expand)
    grad_norm_gain = jnp.sum(grad_scaled_in * normed_in, axis=0)
    grad_in = (
        grad_out.astype(jnp.float32) + norm_back(grad_scaled_in * norm_gain, normed_in, inverse_in)
    ).astype(jnp.bfloat16)
    plans = fold_plans(lax.axis_size("rec"), lax.axis_size("tm"))
    half = channels // 2
    share_project = jnp.concatenate(
        [
            sum_shares(grad_project[:, :half], plans[0]),
            sum_shares(grad_project[:, half:], plans[1]),
        ],
        axis=1,
    )
    share_expand = jnp.concatenate(
        [
            sum_shares(grad_expand[:, index * half : (index + 1) * half], plans[index % 2])
            for index in range(4)
        ],
        axis=1,
    )
    small_sums = sum_everywhere(
        jnp.concatenate([grad_taps, grad_norm_gain[None], grad_conv_gain[None]], axis=0)
    )
    small_sums = (small_sums[:taps_count], small_sums[taps_count], small_sums[taps_count + 1])
    return (
        layer_out[None],
        grad_in[None],
        share_expand,
        share_project,
        small_sums[0],
        small_sums[1],
        small_sums[2],
    )


def solution(mesh):
    return jax.shard_map(
        per_device,
        mesh=mesh,
        in_specs=(
            P("rec", "tm", None),
            P("rec", None, None),
            P("rec"),
            P("rec", "tm", None),
            P(),
            P(),
            P(),
            P(),
            P(),
        ),
        out_specs=(
            P("rec", "tm", None),
            P("rec", "tm", None),
            P("tm", None),
            P("tm", None),
            P(),
            P(),
            P(),
        ),
        check_vma=False,
    )
```
